32 devices in a mesh: ex: 16 (over z, x, core), feat: 2 (over y).
Axes of the slice: x: 2, y: 2, z: 4, core: 2. Of those that a mesh axis runs over, the one named last changes fastest.
Arguments:
- lanczos_basis: bfloat16 [131072, 384], P(('ex', 'feat')), may hold values from -0.3125 to 0.3125
- diagonal: float32 [131072], P(('ex', 'feat')), may hold values from 0.3 to 9
- lanczos_scale: float32 [384], replicated, may hold values from 0.3 to 3
- test_tiles: int32 [64, 16], replicated, may hold values from 0 to 1023, as said below
- test_values: bfloat16 [64, 16, 128], replicated, may hold values from -6 to 6
- train_tiles: int32 [256, 16], P('ex', 'feat'), may hold values from 0 to 1023, as said below
- train_count: int32 [256, 2], P('ex', 'feat'), may hold values from 1 to 8, as said below
- train_values: bfloat16 [256, 16, 16, 128], P('ex', 'feat'), may hold values from -6 to 6
- resid_weight: float32 [4096], P('ex'), may hold values from -1 to 1
Outputs:
- influence: float32 [64, 4096], P('feat', 'ex')
The draws below stay inside these ranges and needn't reach their ends.
Inputs may be any that keep to these rules, and one draw needn't show every extreme that they name: `train_tiles`: tile id j lies in the basis rows of the device whose index along ex+feat (ex slowest) is j // 32; the ids in slots f * 8 to (f + 1) * 8 - 1 of a block lie in rows of devices with feat index f. Among all slots of the blocks of one index of ex on one index of feat, at most 12 ids lie in the rows of any one device. In every draw, for each feat index, some device has 12 live slots naming its rows in the blocks of every index of ex. `train_count`: in every draw some block of every index of ex has all 8 slots live on every index of feat. `test_tiles`: the tile ids of one test example are distinct.
All inputs are finite; a program needn't handle non-finite values.
Results may differ from the reference program's by a relative error of at most 0.0042.
Values may be sent and summed in bfloat16 or wider, within the bound.
No kernel may reach another device: no remote copies, remote signals or barrier semaphores. Data moves between devices by JAX's collectives and lax.ppermute only.
A program may use at most 64 MiB of HBM per device.

```python
import math
import jax
import jax.numpy as jnp
from jax import lax

RANK = 384
TESTS = 64
TT = 16
EB = 16
SLOT_F = 8
BLK_DEV = 16
FEATURES = 131072
NTILES = 1024
TILES_DEV = 32
BLOCKS = 256
TPB = 16
TRAIN = 4096
CAP = 12
N_EX = 16
N_FEAT = 2


def draw_train_tiles(key, part):
    key_hot, key_noise, key_local = jax.random.split(jax.random.fold_in(key, 17), 3)
    slot_total = BLK_DEV * SLOT_F
    cell_total = N_EX * CAP
    hot_owner = jax.random.randint(key_hot, (N_FEAT,), 0, N_EX)
    cell_index = jnp.arange(cell_total, dtype=jnp.int32)
    noise = jax.random.randint(key_noise, (N_EX, N_FEAT, cell_total), 1, 65536)
    hot_cell = cell_index[None, None, :] // CAP == hot_owner[None, :, None]
    ordering = jnp.where(hot_cell, 0, noise) * cell_total + cell_index[None, None, :]
    chosen = jnp.argsort(ordering, axis=-1)[:, :, :slot_total]
    owner_seq = (chosen // CAP).astype(jnp.int32)
    position = jnp.arange(slot_total, dtype=jnp.int32)
    hot_slot = (position % SLOT_F == 0) & (position // SLOT_F < CAP)
    placing = jnp.argsort(jnp.where(hot_slot, 0, 1) * slot_total + position)
    owner_at = jnp.zeros((N_EX, N_FEAT, slot_total), jnp.int32).at[:, :, placing].set(owner_seq)
    local_tile = jax.random.randint(key_local, (N_EX, N_FEAT, slot_total), 0, TILES_DEV)
    column = jnp.arange(N_FEAT, dtype=jnp.int32)[None, :, None]
    tile_id = (owner_at * N_FEAT + column) * TILES_DEV + local_tile
    tile_id = tile_id.reshape(N_EX, N_FEAT, BLK_DEV, SLOT_F).transpose(0, 2, 1, 3)
    return tile_id.reshape(N_EX * BLK_DEV, N_FEAT * SLOT_F).astype(jnp.int32)


def draw_train_count(key, part):
    counts = jax.random.randint(jax.random.fold_in(key, 23), (N_EX * BLK_DEV, N_FEAT), 1, SLOT_F + 1)
    full_row = jnp.arange(N_EX * BLK_DEV) % BLK_DEV == BLK_DEV - 1
    return jnp.where(full_row[:, None], SLOT_F, counts).astype(jnp.int32)


def draw_test_tiles(key, part):
    stride = NTILES // TT
    base = jax.random.randint(jax.random.fold_in(key, 29), (TESTS, TT), 0, stride)
    return (base + jnp.arange(TT, dtype=jnp.int32)[None, :] * stride).astype(jnp.int32)


def draw_diagonal(key, part):
    inner = jax.random.fold_in(key, 31)
    spot = jnp.arange(FEATURES, dtype=jnp.float32) / FEATURES
    base = jnp.exp(jax.random.uniform(inner, (FEATURES,), jnp.float32, math.log(0.3), math.log(3.0)))
    return base * (1.0 + 2.0 * spot)


def shard_levels(stream_key, extent, shards, least, largest):
    factor_of, own = 1.0, jax.random.fold_in(stream_key, 6)
    for axis_at, blocks in shards:
        heights = jnp.exp(jax.random.uniform(jax.random.fold_in(own, axis_at), (blocks,), jnp.float32, least / len(shards), largest / len(shards)))
        factor_of = factor_of * jnp.repeat(heights, extent[axis_at] // blocks).reshape([-1 if axis == axis_at else 1 for axis in range(len(extent))])
    return factor_of


def gaussian(key, extent, scale, limit, cuts=(), held_as=jnp.bfloat16):
    entries = scale * jax.random.normal(key, extent, jnp.float32)
    if cuts:
        entries = entries * shard_levels(key, extent, cuts, -0.22, 0.18)
    return jnp.clip(entries, -limit, limit).astype(held_as)


def setup_inputs(seed: int = 0) -> dict:
    splits = jax.random.split(jax.random.key(seed), 10)
    return {
        "lanczos_basis": gaussian(splits[0], (FEATURES, RANK), RANK ** -0.5, 0.3125, ((0, 32),)),
        "diagonal": draw_diagonal(jax.random.fold_in(splits[9], 71), 0),
        "lanczos_scale": jnp.clip(jnp.exp(jax.random.uniform(splits[2], (RANK,), jnp.float32, math.log(0.3), math.log(3.0))), 0.3, 3.0),
        "test_tiles": draw_test_tiles(jax.random.fold_in(splits[9], 71), 0),
        "test_values": gaussian(splits[4], (TESTS, TT, 128), 1.0, 6.0),
        "train_tiles": draw_train_tiles(jax.random.fold_in(splits[9], 71), 0),
        "train_count": draw_train_count(jax.random.fold_in(splits[9], 71), 0),
        "train_values": gaussian(splits[7], (BLOCKS, TPB, EB, 128), 1.0, 6.0, ((0, 16), (1, 2))),
        "resid_weight": jnp.clip(jax.random.uniform(splits[8], (TRAIN,), jnp.float32, -1.0, 1.0) * shard_levels(splits[8], (TRAIN,), ((0, 16),), -0.4, 0.0), -1.0, 1.0),
    }


def reference(lanczos_basis, diagonal, lanczos_scale, test_tiles, test_values, train_tiles, train_count, train_values, resid_weight):
    test_count = test_tiles.shape[0]
    group_size = 32
    basis_tiles = lanczos_basis.reshape(NTILES, 128, RANK)
    picked = basis_tiles[test_tiles].astype(jnp.float32)
    projection = jnp.einsum('tsfr,tsf->tr', picked, test_values.astype(jnp.float32))
    scaled_proj = (lanczos_scale[None, :] * projection).astype(jnp.bfloat16)
    dense_test = jnp.zeros((NTILES, test_count, 128), jnp.bfloat16)
    dense_test = dense_test.at[test_tiles, jnp.arange(test_count)[:, None]].add(test_values)
    diag_tiles = diagonal.reshape(NTILES, 128)

    def one_group(pieces):
        basis_part, tests_part, diag_part = pieces
        low_rank = jnp.einsum('gfr,tr->gtf', basis_part.astype(jnp.float32), scaled_proj.astype(jnp.float32))
        tests_wide = tests_part.astype(jnp.float32)
        exact_dir = diag_part[:, None, :] * tests_wide + low_rank
        part_self = lax.optimization_barrier(jnp.sum(tests_wide * exact_dir, axis=(0, 2)))
        return (exact_dir.astype(jnp.bfloat16), part_self)
    direction, self_parts = lax.map(one_group, (basis_tiles.reshape(NTILES // group_size, group_size, 128, RANK), dense_test.reshape(NTILES // group_size, group_size, test_count, 128), diag_tiles.reshape(NTILES // group_size, group_size, 128)))
    direction = direction.reshape(NTILES, test_count, 128)
    self_inf = lax.optimization_barrier(jnp.sum(self_parts, axis=0))
    slots_all = train_tiles.shape[1]
    slot_pos = jnp.arange(slots_all) % SLOT_F
    slot_col = jnp.arange(slots_all) // SLOT_F

    def one_block(pieces):
        tile_ids, slot_counts, tile_values = pieces
        slot_live = slot_pos < slot_counts[slot_col]
        fetched = jnp.where(slot_live[:, None, None], direction[tile_ids], jnp.zeros((), jnp.bfloat16))
        return jnp.einsum('jef,jtf->te', tile_values.astype(jnp.float32), fetched.astype(jnp.float32))
    raw_scores = lax.map(one_block, (train_tiles, train_count, train_values))
    blocks = train_tiles.shape[0]
    raw_scores = jnp.transpose(raw_scores, (1, 0, 2)).reshape(test_count, blocks * EB)
    return -resid_weight[None, :] * raw_scores / jnp.sqrt(self_inf)[:, None]
```

```python
import functools

import jax
import jax.numpy as jnp
from jax import lax
from jax.experimental import pallas as pl
from jax.experimental.pallas import tpu as pltpu
from jax.sharding import PartitionSpec as P


LANES = 128
BOTH = ("ex", "feat")
NT = (((1,), (1,)), ((), ()))


def pack_kernel(tiles_per_owner, tiles_here, cap, examples, tiles_ref, count_ref, values_ref, send_ref, block_ref, fill_ref):
    blocks_here, slots_here = tiles_ref.shape
    owners = send_ref.shape[0]
    send_ref[...] = jnp.zeros_like(send_ref)
    for owner in range(owners):
        fill_ref[owner] = 0
        for place in range(cap):
            block_ref[owner, place] = -1
    rows = lax.broadcasted_iota(jnp.int32, (owners, LANES), 0)
    lanes = lax.broadcasted_iota(jnp.int32, (owners, LANES), 1)

    def one_block(block, ids):
        count = count_ref[block, 0]
        for slot in range(slots_here):
            tile = tiles_ref[block, slot]
            owner = tile // tiles_per_owner
            live = slot < count
            place = fill_ref[owner]

            @pl.when(live)
            def _():
                start = pl.multiple_of(place * examples, examples)
                source = pl.multiple_of((block * slots_here + slot) * examples, examples)
                send_ref[owner, pl.ds(start, examples), :] = values_ref[pl.ds(source, examples), :]
                block_ref[owner, place] = block
                fill_ref[owner] = place + 1

            hit = (rows == owner) & (lanes == place) & live
            ids = jnp.where(hit, (tile % tiles_here).astype(jnp.float32), ids)
        return ids

    ids = lax.fori_loop(0, blocks_here, one_block, jnp.zeros((owners, LANES), jnp.float32))
    for owner in range(owners):
        send_ref[owner, cap * examples :, :] = jnp.broadcast_to(
            ids[owner : owner + 1, :], (examples, LANES)
        ).astype(jnp.bfloat16)


def direction_kernel(tiles, basis_ref, scaled_ref, test_ref, diag_ref, out_ref):
    for tile in range(tiles):
        low_rank = lax.dot_general(
            scaled_ref[...], basis_ref[tile], NT, preferred_element_type=jnp.float32
        )
        wide = test_ref[tile].astype(jnp.float32)
        out_ref[tile] = (diag_ref[tile : tile + 1, :] * wide + low_rank).astype(jnp.bfloat16)


def score_kernel(cap, examples, groups, ids_ref, recv_ref, dir_ref, out_ref, acc_ref):
    peers, feats, out_rows, _ = out_ref.shape
    tests_here = LANES // groups

    def one_peer(peer, carry):
        for place in range(cap):
            got = lax.dot_general(
                recv_ref[peer, place * examples : (place + 1) * examples, :],
                dir_ref[ids_ref[peer, place]],
                NT,
                preferred_element_type=jnp.float32,
            )
            acc_ref[place * examples : (place + 1) * examples, :] = got
        parts = [acc_ref[pl.ds(k, out_rows, stride=groups), :] for k in range(groups)]
        for feat in range(feats):
            lanes = slice(feat * tests_here, (feat + 1) * tests_here)
            out_ref[peer, feat] = jnp.concatenate([part[:, lanes] for part in parts], axis=1).astype(
                jnp.bfloat16
            )
        return carry

    lax.fori_loop(0, peers, one_peer, 0)


def xor_permute(value, axes, size, offset):
    return lax.ppermute(value, axes, [(i, i ^ offset) for i in range(size)])


def all_sum(value, total, core_bit):
    core = (lax.axis_index(BOTH) // core_bit) % 2
    mine = lax.dynamic_index_in_dim(value, core, 0, keepdims=False)
    other = lax.dynamic_index_in_dim(value, 1 - core, 0, keepdims=False)
    part = mine + xor_permute(other, BOTH, total, core_bit)
    bits = [1 << b for b in range(total.bit_length() - 1) if (1 << b) != core_bit]
    while bits:
        stage, bits = bits[:2], bits[2:]
        if len(stage) == 2:
            low, high = stage
            a = xor_permute(part, BOTH, total, low)
            b = xor_permute(part, BOTH, total, high)
            c = xor_permute(part, BOTH, total, low | high)
            part = (part + a) + (b + c)
        else:
            part = part + xor_permute(part, BOTH, total, stage[0])
    other = xor_permute(part, BOTH, total, core_bit)
    low = jnp.where(core == 0, part, other)
    high = jnp.where(core == 0, other, part)
    return low, high


def body(
    lanczos_basis,
    diagonal,
    lanczos_scale,
    test_tiles,
    test_values,
    train_tiles,
    train_count,
    train_values,
    resid_weight,
):
    ex_devices = lax.axis_size("ex")
    feat_devices = lax.axis_size("feat")
    total = ex_devices * feat_devices
    rank = lanczos_basis.shape[1]
    tiles_here = lanczos_basis.shape[0] // LANES
    test_count, test_slots = test_tiles.shape
    tests_here = test_count // feat_devices
    blocks_here, slots_here, examples, _ = train_values.shape
    slot_total = blocks_here * slots_here
    cap = max(2, (3 * slot_total + 2 * ex_devices - 1) // (2 * ex_devices))
    groups = LANES // tests_here
    rows_slot = examples // groups
    vmem = pl.BlockSpec(memory_space=pltpu.VMEM)
    smem = pl.BlockSpec(memory_space=pltpu.SMEM)

    send, block_of = pl.pallas_call(
        functools.partial(pack_kernel, tiles_here * feat_devices, tiles_here, cap, examples),
        out_shape=(
            jax.ShapeDtypeStruct((ex_devices, (cap + 1) * examples, LANES), jnp.bfloat16),
            jax.ShapeDtypeStruct((ex_devices, cap), jnp.int32),
        ),
        in_specs=[smem, smem, vmem],
        out_specs=(vmem, smem),
        scratch_shapes=[pltpu.SMEM((ex_devices,), jnp.int32)],
        name="pack",
    )(train_tiles, train_count, train_values.reshape(slot_total * examples, LANES))
    recv = lax.all_to_all(send, "ex", split_axis=0, concat_axis=0, tiled=True)
    ids = recv[:, cap * examples, :cap].astype(jnp.int32)

    first_tile = lax.axis_index(BOTH) * tiles_here
    offsets = test_tiles - first_tile
    matches = (offsets[None, :, :] == jnp.arange(tiles_here)[:, None, None]).astype(jnp.bfloat16)
    local_test = jnp.einsum(
        "ats,tsf->atf", matches, test_values, preferred_element_type=jnp.float32
    ).astype(jnp.bfloat16)
    basis_tiles = lanczos_basis.reshape(tiles_here, LANES, rank)
    diag_tiles = diagonal.reshape(tiles_here, LANES)
    partial_proj = jnp.einsum(
        "afr,atf->tr", basis_tiles, local_test, preferred_element_type=jnp.float32
    )
    test_wide = local_test.astype(jnp.float32)
    partial_self = jnp.sum(diag_tiles[:, None, :] * test_wide * test_wide, axis=(0, 2))
    half = test_count // 2
    extra = jnp.pad(partial_self.reshape(2, 1, half), ((0, 0), (0, 7), (0, rank - half)))
    payload = jnp.concatenate([partial_proj.reshape(2, half, rank), extra], axis=1)
    low, high = all_sum(payload, total, feat_devices)
    projection = jnp.concatenate([low[:half], high[:half]], axis=0)
    scaled = (lanczos_scale[None, :] * projection).astype(jnp.bfloat16)
    self_inf = jnp.concatenate([low[half, :half], high[half, :half]]) + jnp.sum(
        projection * scaled.astype(jnp.float32), axis=1
    )

    direction = pl.pallas_call(
        functools.partial(direction_kernel, tiles_here),
        out_shape=jax.ShapeDtypeStruct((tiles_here, test_count, LANES), jnp.bfloat16),
        in_specs=[vmem] * 4,
        out_specs=vmem,
        name="direction",
    )(basis_tiles, scaled, local_test, diag_tiles)

    scores = pl.pallas_call(
        functools.partial(score_kernel, cap, examples, groups),
        out_shape=jax.ShapeDtypeStruct(
            (ex_devices, feat_devices, cap * rows_slot, LANES), jnp.bfloat16
        ),
        in_specs=[smem, vmem, vmem],
        out_specs=vmem,
        scratch_shapes=[pltpu.VMEM((cap * examples, test_count), jnp.float32)],
        name="scores",
    )(ids, recv, direction)
    scores = scores.reshape(total, cap * rows_slot, LANES)
    back = lax.all_to_all(scores, BOTH, split_axis=0, concat_axis=0, tiled=True)

    feat_index = lax.axis_index("feat")
    blocks_by_feat = [block_of] + [
        xor_permute(block_of, "feat", feat_devices, k) for k in range(1, feat_devices)
    ]
    stacked = jnp.stack(blocks_by_feat)
    order = jnp.arange(feat_devices) ^ feat_index
    table = jnp.sum(
        jnp.where(
            (order[:, None] == jnp.arange(feat_devices)[None, :])[:, :, None, None],
            stacked[:, None],
            0,
        ),
        axis=0,
    )
    table = table.transpose(1, 0, 2).reshape(total * cap)
    row = jnp.arange(total * cap * rows_slot)
    want = jnp.repeat(table, rows_slot) * rows_slot + row % rows_slot
    want = jnp.where(jnp.repeat(table, rows_slot) < 0, -1, want)
    onehot = (jnp.arange(blocks_here * rows_slot)[:, None] == want[None, :]).astype(jnp.bfloat16)
    raw = jnp.dot(
        onehot, back.reshape(total * cap * rows_slot, LANES), preferred_element_type=jnp.float32
    )
    raw = raw.reshape(blocks_here * rows_slot, groups, tests_here).transpose(2, 0, 1)
    raw = raw.reshape(tests_here, blocks_here * examples)
    self_mine = lax.dynamic_slice_in_dim(self_inf, feat_index * tests_here, tests_here)
    return -resid_weight[None, :] * raw / jnp.sqrt(self_mine)[:, None]


def solution(mesh):
    return jax.shard_map(
        body,
        mesh=mesh,
        in_specs=(
            P(("ex", "feat"), None),
            P(("ex", "feat")),
            P(),
            P(),
            P(),
            P("ex", "feat"),
            P("ex", "feat"),
            P("ex", "feat", None, None),
            P("ex"),
        ),
        out_specs=P("feat", "ex"),
        check_vma=False,
    )
```

```python
import functools

import jax
import jax.numpy as jnp
from jax import lax
from jax.experimental import pallas as pl
from jax.experimental.pallas import tpu as pltpu
from jax.sharding import PartitionSpec as P


LANES = 128
BOTH = ("ex", "feat")
VMEM_LIMIT = 16 << 20
SMALL_LIMIT = 4 << 20


def divide(value, by):
    if by & (by - 1) == 0:
        return lax.shift_right_logical(value, by.bit_length() - 1)
    return lax.div(value, by)


def pack_kernel(
    sizes, tiles_ref, count_ref, values_ref, send_ref, want_ref, fill_ref
):
    tiles_per_owner, tiles_here, cap, examples, rows_slot = sizes
    slots_here, blocks_here = tiles_ref.shape
    owners = send_ref.shape[0]
    rank = want_ref.shape[1]
    send_ref[...] = jnp.zeros_like(send_ref)
    for owner in range(owners):
        fill_ref[owner] = 0
    rows = lax.broadcasted_iota(jnp.int32, (owners, LANES), 0) * LANES
    lanes = lax.broadcasted_iota(jnp.int32, (owners, LANES), 1)
    id_key = rows + lanes
    want_key = rows + divide(lanes, rows_slot)
    want_low = (lanes - divide(lanes, rows_slot) * rows_slot).astype(jnp.float32)

    def one_block(block, carry):
        ids, want = carry
        count = count_ref[0, block]
        for slot in range(slots_here):
            tile = tiles_ref[slot, block]
            owner = divide(tile, tiles_per_owner)
            live = slot < count
            place = fill_ref[owner]
            fill_ref[owner] = place + live.astype(jnp.int32)
            place = jnp.where(live, place, cap)
            start = pl.multiple_of(place * examples, examples)
            source = pl.multiple_of((block * slots_here + slot) * examples, examples)
            send_ref[owner, pl.ds(start, examples), :] = values_ref[pl.ds(source, examples), :]
            key = owner * LANES + place
            local = tile - divide(tile, tiles_here) * tiles_here
            ids = jnp.where(id_key == key, local.astype(jnp.float32), ids)
            want = jnp.where(want_key == key, (block * rows_slot).astype(jnp.float32), want)
        return ids, want

    blank = jnp.full((owners, LANES), -float(LANES * LANES), jnp.float32)
    ids, want = lax.fori_loop(
        0, blocks_here, one_block, (jnp.zeros((owners, LANES), jnp.float32), blank)
    )
    for owner in range(owners):
        send_ref[owner, cap * examples :, :] = jnp.broadcast_to(
            ids[owner : owner + 1, :], (examples, LANES)
        ).astype(jnp.bfloat16)
    want = jnp.where(want_key - rows < cap, want + want_low, blank)
    want_ref[...] = jnp.concatenate([want] + [blank] * (rank // LANES - 1), axis=1)


def device_place(tiles_here):
    ex, feat, feats = lax.axis_index("ex"), lax.axis_index("feat"), lax.axis_size("feat")
    return (ex * feats + feat) * tiles_here, ex % 2


def project_kernel(
    chunk, tests_hbm, diag_hbm, test_hbm, basis_hbm, mine_hbm, other_hbm, local_hbm,
    tests_ref, diag_ref, test_ref, basis_ref, mine_ref, other_ref, local_ref, flat_ref, sems, chunk_sems,
):
    small_copies = [
        pltpu.make_async_copy(source, target, sems.at[i])
        for i, (source, target) in enumerate(
            ((tests_hbm, tests_ref), (test_hbm, test_ref), (diag_hbm, diag_ref))
        )
    ]
    for copy in small_copies:
        copy.start()
    basis_copies = []
    for i in range(chunk_sems.shape[0]):
        window = pl.ds(i * chunk, chunk)
        copy = pltpu.make_async_copy(basis_hbm.at[window], basis_ref.at[window], chunk_sems.at[i])
        copy.start()
        basis_copies.append(copy)
    tiles_here = local_ref.shape[0]
    test_slots, tests = tests_ref.shape
    rank = basis_ref.shape[1]
    half = tests // 2
    first_tile, core = device_place(tiles_here)
    small_copies[0].wait()
    offset = tests_ref[...] - first_tile
    offset = jnp.where((offset >= 0) & (offset < tiles_here), offset, -1)
    offset = offset.astype(jnp.float32).T.astype(jnp.bfloat16)
    width = tests * test_slots
    column = lax.broadcasted_iota(jnp.int32, (test_slots, width), 1)
    spread = column - divide(column, test_slots) * test_slots == lax.broadcasted_iota(
        jnp.int32, (test_slots, width), 0
    )
    named = jnp.dot(
        offset, spread.astype(jnp.float32).astype(jnp.bfloat16), preferred_element_type=jnp.float32
    )
    own = divide(lax.broadcasted_iota(jnp.int32, (tests, width), 1), test_slots) == (
        lax.broadcasted_iota(jnp.int32, (tests, width), 0)
    )
    named = jnp.where(own, named, -1.0)
    small_copies[1].wait()
    small_copies[2].wait()
    influence = jnp.zeros((tests, LANES), jnp.float32)
    group = min(8, tiles_here)
    for begin in range(0, tiles_here, group):
        pick = jnp.concatenate(
            [
                jnp.where(named == float(tile), 1.0, 0.0).astype(jnp.bfloat16)
                for tile in range(begin, begin + group)
            ],
            axis=0,
        )
        got = jnp.dot(pick, test_ref[...], preferred_element_type=jnp.float32)
        for tile in range(begin, begin + group):
            wide = got[(tile - begin) * tests : (tile - begin + 1) * tests, :]
            narrow = wide.astype(jnp.bfloat16)
            local_ref[tile] = narrow
            flat_ref[:, tile * LANES : (tile + 1) * LANES] = narrow
            influence = influence + diag_ref[tile : tile + 1, :] * wide * wide

    local_copy = pltpu.make_async_copy(local_ref, local_hbm, sems.at[3])
    local_copy.start()
    projection = jnp.zeros((tests, rank), jnp.float32)
    for i, copy in enumerate(basis_copies):
        begin = i * chunk
        copy.wait()
        projection = projection + jnp.dot(
            flat_ref[:, begin : begin + chunk],
            basis_ref[begin : begin + chunk, :],
            preferred_element_type=jnp.float32,
        )
    total = jnp.sum(influence, axis=1, keepdims=True)
    eye = lax.broadcasted_iota(jnp.int32, (half, LANES), 0) == lax.broadcasted_iota(
        jnp.int32, (half, LANES), 1
    )
    row = [
        jnp.sum(jnp.where(eye, total[i * half : (i + 1) * half], 0.0), axis=0, keepdims=True)
        for i in range(2)
    ]
    first = core == 0
    out_copies = [local_copy]
    for ref, out_hbm, a, b in ((other_ref, other_hbm, 1, 0), (mine_ref, mine_hbm, 0, 1)):
        ref[:half, :] = jnp.where(
            first, projection[a * half : (a + 1) * half], projection[b * half : (b + 1) * half]
        )
        ref[half:, :] = jnp.zeros((8, rank), jnp.float32)
        ref[half : half + 1, :LANES] = jnp.where(first, row[a], row[b])
        copy = pltpu.make_async_copy(ref, out_hbm, sems.at[4 + a])
        copy.start()
        out_copies.append(copy)
    for copy in out_copies:
        copy.wait()


def hold_kernel(in_ref, out_ref):
    out_ref[...] = in_ref[...]


def pair_kernel(mine_ref, got_ref, rider_ref, part_ref, both_ref):
    rows = mine_ref.shape[0]
    part = mine_ref[...] + got_ref[...]
    part_ref[...] = part
    both_ref[:rows, :] = part
    both_ref[rows:, :] = rider_ref[...]


def quad_kernel(mine_ref, a_ref, b_ref, c_ref, part_ref):
    rows = mine_ref.shape[0]
    part_ref[...] = (mine_ref[...] + a_ref[:rows, :]) + (b_ref[...] + c_ref[...])


def small_call(kernel, shapes, *args, name):
    vmem = pl.BlockSpec(memory_space=pltpu.VMEM)
    return pl.pallas_call(
        kernel,
        out_shape=tuple(jax.ShapeDtypeStruct(shape, dtype) for shape, dtype in shapes),
        in_specs=[vmem] * len(args),
        out_specs=(vmem,) * len(shapes),
        compiler_params=pltpu.CompilerParams(vmem_limit_bytes=SMALL_LIMIT),
        name=name,
    )(*args)


def score_kernel(
    cap, examples, groups, chunk,
    part_ref, other_ref, scale_ref, diag_ref, test_ref, basis_ref, recv_ref,
    out_hbm, self_ref,
    dir_ref, acc_ref, out_ref, tile_ref, ids_ref, ids_sem, out_sems,
):
    peers, feats, out_rows, _ = out_ref.shape
    tests_here = LANES // groups
    half = part_ref.shape[0] - 8
    tests = 2 * half
    tiles = dir_ref.shape[0]
    starts = list(range(0, tiles, chunk))
    for peer in range(peers):
        row = recv_ref[peer, cap * examples : (cap + 1) * examples, :].astype(jnp.float32)
        tile_ref[peer : peer + 1, :] = row[:1, :].astype(jnp.int32)
    fetch = pltpu.make_async_copy(tile_ref, ids_ref, ids_sem)
    fetch.start()
    first = device_place(tiles)[1] == 0
    low = jnp.where(first, part_ref[...], other_ref[...])
    high = jnp.where(first, other_ref[...], part_ref[...])
    projection = jnp.concatenate([low[:half], high[:half]], axis=0)
    scaled = (scale_ref[...][None, :] * projection).astype(jnp.bfloat16)
    low_rank = jnp.sum(projection * scaled.astype(jnp.float32), axis=1, keepdims=True)
    eye = lax.broadcasted_iota(jnp.int32, (half, half), 0) == lax.broadcasted_iota(
        jnp.int32, (half, half), 1
    )
    diagonal = [
        jnp.sum(jnp.where(eye, piece[half : half + 1, :half], 0.0), axis=1, keepdims=True)
        for piece in (low, high)
    ]
    self_ref[...] = jnp.broadcast_to(
        low_rank + jnp.concatenate(diagonal, axis=0), (tests, LANES)
    )
    weights = scaled.T
    diag = diag_ref[...].T

    def directions(i):
        begin = starts[i]
        got = jnp.dot(
            basis_ref[begin * LANES : (begin + chunk) * LANES, :],
            weights,
            preferred_element_type=jnp.float32,
        )
        for tile in range(begin, begin + chunk):
            wide = test_ref[tile].astype(jnp.float32).T
            low_part = got[(tile - begin) * LANES : (tile - begin + 1) * LANES, :]
            dir_ref[tile] = (diag[:, tile : tile + 1] * wide + low_part).astype(jnp.bfloat16)

    for i in range(len(starts)):
        directions(i)
    fetch.wait()

    waves, unroll = out_sems.shape[0], acc_ref.shape[0]

    def some_peers(step, carry):
        for i in range(unroll):
            peer = step * unroll + i
            for place in range(cap):
                acc_ref[i, place * examples : (place + 1) * examples, :] = jnp.dot(
                    recv_ref[peer, place * examples : (place + 1) * examples, :],
                    dir_ref[ids_ref[peer, place]],
                    preferred_element_type=jnp.float32,
                )
        for i in range(unroll):
            peer = step * unroll + i
            parts = [acc_ref[i, pl.ds(k, out_rows, stride=groups), :] for k in range(groups)]
            for feat in range(feats):
                lanes = slice(feat * tests_here, (feat + 1) * tests_here)
                out_ref[peer, feat] = jnp.concatenate(
                    [part[:, lanes] for part in parts], axis=1
                ).astype(jnp.bfloat16)
        return carry

    per_wave = peers // waves
    out_copies = []
    for i in range(waves):
        lax.fori_loop(i * per_wave // unroll, (i + 1) * per_wave // unroll, some_peers, 0)
        window = pl.ds(i * per_wave, per_wave)
        copy = pltpu.make_async_copy(out_ref.at[window], out_hbm.at[window], out_sems.at[i])
        copy.start()
        out_copies.append(copy)
    for copy in out_copies:
        copy.wait()


def xor_permute(value, axes, size, offset):
    return lax.ppermute(value, axes, [(i, i ^ offset) for i in range(size)])


def all_sum(mine, other, total, core_bit, rider):
    wide = jnp.float32
    got = xor_permute(other, BOTH, total, core_bit)
    shape = mine.shape
    (mine,) = small_call(hold_kernel, [(shape, wide)], mine, name="hold")
    part, send = small_call(
        pair_kernel,
        [(shape, wide), ((shape[0] + rider.shape[0], shape[1]), wide)],
        mine,
        got,
        rider,
        name="pair",
    )
    bits = [1 << b for b in range(total.bit_length() - 1) if (1 << b) != core_bit]
    arrived = None
    while bits:
        low, high = bits[:2] if len(bits) > 1 else (bits[0], 0)
        bits = bits[2:]
        a = xor_permute(send if arrived is None else part, BOTH, total, low)
        if arrived is None:
            arrived = a[shape[0] :]
        if high:
            b = xor_permute(part, BOTH, total, high)
            c = xor_permute(part, BOTH, total, low | high)
        else:
            b = c = jnp.zeros(shape, wide)
        (part,) = small_call(quad_kernel, [(shape, wide)], part, a, b, c, name="quad")
    return part, xor_permute(part, BOTH, total, core_bit), arrived


def body(
    lanczos_basis,
    diagonal,
    lanczos_scale,
    test_tiles,
    test_values,
    train_tiles,
    train_count,
    train_values,
    resid_weight,
):
    ex_devices = lax.axis_size("ex")
    feat_devices = lax.axis_size("feat")
    total = ex_devices * feat_devices
    rank = lanczos_basis.shape[1]
    tiles_here = lanczos_basis.shape[0] // LANES
    test_count, test_slots = test_tiles.shape
    tests_here = test_count // feat_devices
    blocks_here, slots_here, examples, _ = train_values.shape
    slot_total = blocks_here * slots_here
    cap = max(2, (3 * slot_total + 2 * ex_devices - 1) // (2 * ex_devices))
    groups = LANES // tests_here
    rows_slot = examples // groups
    vmem = pl.BlockSpec(memory_space=pltpu.VMEM)
    smem = pl.BlockSpec(memory_space=pltpu.SMEM)
    hbm = pl.BlockSpec(memory_space=pltpu.HBM)
    params = pltpu.CompilerParams(vmem_limit_bytes=VMEM_LIMIT)

    sizes = (tiles_here * feat_devices, tiles_here, cap, examples, rows_slot)
    send_shape = (ex_devices, (cap + 1) * examples, LANES)
    send, want = pl.pallas_call(
        functools.partial(pack_kernel, sizes),
        out_shape=(
            jax.ShapeDtypeStruct(send_shape, jnp.bfloat16),
            jax.ShapeDtypeStruct((ex_devices, rank), jnp.float32),
        ),
        in_specs=[smem, smem, vmem],
        out_specs=(vmem, vmem),
        scratch_shapes=[pltpu.SMEM((ex_devices,), jnp.int32)],
        name="pack",
    )(train_tiles.T, train_count.T, train_values.reshape(slot_total * examples, LANES))
    recv = lax.all_to_all(send, "ex", split_axis=0, concat_axis=0, tiled=True)

    half = test_count // 2
    diag_tiles = diagonal.reshape(tiles_here, LANES)
    part_shape = (half + 8, rank)
    local_shape = (tiles_here, test_count, LANES)
    mine, other, local_test = pl.pallas_call(
        functools.partial(project_kernel, min(8, tiles_here) * LANES),
        out_shape=(
            jax.ShapeDtypeStruct(part_shape, jnp.float32),
            jax.ShapeDtypeStruct(part_shape, jnp.float32),
            jax.ShapeDtypeStruct(local_shape, jnp.bfloat16),
        ),
        in_specs=[hbm] * 4,
        out_specs=(hbm,) * 3,
        scratch_shapes=[
            pltpu.VMEM((test_slots, test_count), jnp.int32),
            pltpu.VMEM((tiles_here, LANES), jnp.float32),
            pltpu.VMEM((test_count * test_slots, LANES), jnp.bfloat16),
            pltpu.VMEM(lanczos_basis.shape, jnp.bfloat16),
            pltpu.VMEM(part_shape, jnp.float32),
            pltpu.VMEM(part_shape, jnp.float32),
            pltpu.VMEM(local_shape, jnp.bfloat16),
            pltpu.VMEM((test_count, tiles_here * LANES), jnp.bfloat16),
            pltpu.SemaphoreType.DMA((6,)),
            pltpu.SemaphoreType.DMA((tiles_here // min(8, tiles_here),)),
        ],
        name="project",
    )(
        test_tiles.T,
        diag_tiles,
        test_values.reshape(test_count * test_slots, LANES),
        lanczos_basis,
    )
    part, other, arrived = all_sum(mine, other, total, feat_devices, want)

    local_test, recv = lax.optimization_barrier((local_test, recv))

    out_shape = (ex_devices, feat_devices, cap * rows_slot, LANES)
    waves = min(4, ex_devices)
    scores, self_wide = pl.pallas_call(
        functools.partial(score_kernel, cap, examples, groups, min(4, tiles_here)),
        out_shape=(
            jax.ShapeDtypeStruct(out_shape, jnp.bfloat16),
            jax.ShapeDtypeStruct((test_count, LANES), jnp.float32),
        ),
        in_specs=[vmem] * 7,
        out_specs=(hbm, vmem),
        scratch_shapes=[
            pltpu.VMEM((tiles_here, LANES, test_count), jnp.bfloat16),
            pltpu.VMEM((2, cap * examples, test_count), jnp.float32),
            pltpu.VMEM(out_shape, jnp.bfloat16),
            pltpu.VMEM((ex_devices, LANES), jnp.int32),
            pltpu.SMEM((ex_devices, LANES), jnp.int32),
            pltpu.SemaphoreType.DMA,
            pltpu.SemaphoreType.DMA((waves,)),
        ],
        compiler_params=params,
        name="scores",
    )(part, other, lanczos_scale, diag_tiles, local_test, lanczos_basis, recv)
    self_inf = self_wide[:, 0]
    scores = scores.reshape(total, cap * rows_slot, LANES)
    back = lax.all_to_all(scores, BOTH, split_axis=0, concat_axis=0, tiled=True)

    feat_index = lax.axis_index("feat")
    out_rows = cap * rows_slot
    want = want[:, :out_rows]
    if feat_devices == 2:
        theirs = arrived[:, :out_rows]
        mine_first = feat_index == 0
        table = jnp.stack(
            [jnp.where(mine_first, want, theirs), jnp.where(mine_first, theirs, want)], axis=1
        )
    else:
        table = lax.all_gather(want, "feat", axis=1)
    table = table.reshape(total * out_rows)
    places = jnp.arange(blocks_here * rows_slot, dtype=jnp.float32)
    onehot = (places[:, None] == table[None, :]).astype(jnp.bfloat16)
    raw = jnp.dot(
        onehot, back.reshape(total * cap * rows_slot, LANES), preferred_element_type=jnp.float32
    )
    raw = raw.reshape(blocks_here * rows_slot, groups, tests_here).transpose(2, 0, 1)
    raw = raw.reshape(tests_here, blocks_here * examples)
    self_mine = lax.dynamic_slice_in_dim(self_inf, feat_index * tests_here, tests_here)
    return -resid_weight[None, :] * raw / jnp.sqrt(self_mine)[:, None]


def solution(mesh):
    return jax.shard_map(
        body,
        mesh=mesh,
        in_specs=(
            P(("ex", "feat"), None),
            P(("ex", "feat")),
            P(),
            P(),
            P(),
            P("ex", "feat"),
            P("ex", "feat"),
            P("ex", "feat", None, None),
            P("ex"),
        ),
        out_specs=P("feat", "ex"),
        check_vma=False,
    )
```

```python
import functools

import jax
import jax.numpy as jnp
from jax import lax
from jax.experimental import pallas as pl
from jax.experimental.pallas import tpu as pltpu
from jax.sharding import PartitionSpec as P


LANES = 128
BOTH = ("ex", "feat")
VMEM_LIMIT = 16 << 20
SMALL_LIMIT = 4 << 20


def divide(value, by):
    if by & (by - 1) == 0:
        return lax.shift_right_logical(value, by.bit_length() - 1)
    return lax.div(value, by)


def pack_kernel(
    sizes, tiles_ref, count_ref, values_ref, send_ref, want_ref, fill_ref
):
    tiles_per_owner, tiles_here, cap, examples, rows_slot = sizes
    slots_here, blocks_here = tiles_ref.shape
    owners = send_ref.shape[0]
    rank = want_ref.shape[1]
    send_ref[...] = jnp.zeros_like(send_ref)
    for owner in range(owners):
        fill_ref[owner] = 0
    rows = lax.broadcasted_iota(jnp.int32, (owners, LANES), 0) * LANES
    lanes = lax.broadcasted_iota(jnp.int32, (owners, LANES), 1)
    id_key = rows + lanes
    want_key = rows + divide(lanes, rows_slot)
    want_low = (lanes - divide(lanes, rows_slot) * rows_slot).astype(jnp.float32)

    def one_block(block, carry):
        ids, want = carry
        count = count_ref[0, block]
        for slot in range(slots_here):
            tile = tiles_ref[slot, block]
            owner = divide(tile, tiles_per_owner)
            live = slot < count
            place = fill_ref[owner]
            fill_ref[owner] = place + live.astype(jnp.int32)
            start = pl.multiple_of(place * examples, examples)
            source = pl.multiple_of((block * slots_here + slot) * examples, examples)
            send_ref[owner, pl.ds(start, examples), :] = values_ref[pl.ds(source, examples), :]
            key = owner * LANES + place
            local = tile - divide(tile, tiles_here) * tiles_here
            ids = jnp.where(id_key == key, local.astype(jnp.float32), ids)
            want = jnp.where((want_key == key) & live, (block * rows_slot).astype(jnp.float32), want)
        return ids, want

    blank = jnp.full((owners, LANES), -float(LANES * LANES), jnp.float32)
    ids, want = lax.fori_loop(
        0, blocks_here, one_block, (jnp.zeros((owners, LANES), jnp.float32), blank)
    )
    for owner in range(owners):
        send_ref[owner, cap * examples :, :] = jnp.broadcast_to(
            ids[owner : owner + 1, :], (8, LANES)
        ).astype(jnp.bfloat16)
    want = jnp.where(want_key - rows < cap, want + want_low, blank)
    want_ref[...] = jnp.concatenate([want] + [blank] * (rank // LANES - 1), axis=1)


def device_place(tiles_here):
    ex, feat, feats = lax.axis_index("ex"), lax.axis_index("feat"), lax.axis_size("feat")
    return (ex * feats + feat) * tiles_here, ex % 2


def project_kernel(
    chunk, tests_hbm, diag_hbm, test_hbm, basis_hbm, mine_hbm, other_hbm, local_hbm,
    tests_ref, diag_ref, test_ref, basis_ref, mine_ref, other_ref, local_ref, flat_ref, sems, chunk_sems,
):
    small_copies = [
        pltpu.make_async_copy(source, target, sems.at[i])
        for i, (source, target) in enumerate(
            ((tests_hbm, tests_ref), (test_hbm, test_ref), (diag_hbm, diag_ref))
        )
    ]
    for copy in small_copies:
        copy.start()
    basis_copies = []
    for i in range(chunk_sems.shape[0]):
        window = pl.ds(i * chunk, chunk)
        copy = pltpu.make_async_copy(basis_hbm.at[window], basis_ref.at[window], chunk_sems.at[i])
        copy.start()
        basis_copies.append(copy)
    tiles_here = local_ref.shape[0]
    test_slots, tests = tests_ref.shape
    rank = basis_ref.shape[1]
    half = tests // 2
    first_tile, core = device_place(tiles_here)
    small_copies[0].wait()
    offset = tests_ref[...] - first_tile
    offset = jnp.where((offset >= 0) & (offset < tiles_here), offset, -1)
    offset = offset.astype(jnp.float32).T.astype(jnp.bfloat16)
    width = tests * test_slots
    column = lax.broadcasted_iota(jnp.int32, (test_slots, width), 1)
    spread = column - divide(column, test_slots) * test_slots == lax.broadcasted_iota(
        jnp.int32, (test_slots, width), 0
    )
    named = jnp.dot(
        offset, spread.astype(jnp.float32).astype(jnp.bfloat16), preferred_element_type=jnp.float32
    )
    own = divide(lax.broadcasted_iota(jnp.int32, (tests, width), 1), test_slots) == (
        lax.broadcasted_iota(jnp.int32, (tests, width), 0)
    )
    named = jnp.where(own, named, -1.0)
    small_copies[1].wait()
    small_copies[2].wait()
    influence = jnp.zeros((tests, LANES), jnp.float32)
    group = min(8, tiles_here)
    for begin in range(0, tiles_here, group):
        pick = jnp.concatenate(
            [
                jnp.where(named == float(tile), 1.0, 0.0).astype(jnp.bfloat16)
                for tile in range(begin, begin + group)
            ],
            axis=0,
        )
        got = jnp.dot(pick, test_ref[...], preferred_element_type=jnp.float32)
        for tile in range(begin, begin + group):
            wide = got[(tile - begin) * tests : (tile - begin + 1) * tests, :]
            narrow = wide.astype(jnp.bfloat16)
            local_ref[tile] = narrow
            flat_ref[:, tile * LANES : (tile + 1) * LANES] = narrow
            influence = influence + diag_ref[tile : tile + 1, :] * wide * wide

    local_copy = pltpu.make_async_copy(local_ref, local_hbm, sems.at[3])
    local_copy.start()
    projection = jnp.zeros((tests, rank), jnp.float32)
    for i, copy in enumerate(basis_copies):
        begin = i * chunk
        copy.wait()
        projection = projection + jnp.dot(
            flat_ref[:, begin : begin + chunk],
            basis_ref[begin : begin + chunk, :],
            preferred_element_type=jnp.float32,
        )
    total = jnp.sum(influence, axis=1, keepdims=True)
    eye = lax.broadcasted_iota(jnp.int32, (half, LANES), 0) == lax.broadcasted_iota(
        jnp.int32, (half, LANES), 1
    )
    row = [
        jnp.sum(jnp.where(eye, total[i * half : (i + 1) * half], 0.0), axis=0, keepdims=True)
        for i in range(2)
    ]
    first = core == 0
    out_copies = [local_copy]
    for ref, out_hbm, a, b in ((other_ref, other_hbm, 1, 0), (mine_ref, mine_hbm, 0, 1)):
        ref[:half, :] = jnp.where(
            first, projection[a * half : (a + 1) * half], projection[b * half : (b + 1) * half]
        )
        ref[half:, :] = jnp.zeros((8, rank), jnp.float32)
        ref[half : half + 1, :LANES] = jnp.where(first, row[a], row[b])
        copy = pltpu.make_async_copy(ref, out_hbm, sems.at[4 + a])
        copy.start()
        out_copies.append(copy)
    for copy in out_copies:
        copy.wait()


def add_kernel(mine_ref, got_ref, part_ref):
    part_ref[...] = mine_ref[...] + got_ref[...]


def hold_kernel(in_ref, out_ref):
    out_ref[...] = in_ref[...]


def pair_kernel(mine_ref, got_ref, rider_ref, part_ref, both_ref):
    rows = mine_ref.shape[0]
    part = mine_ref[...] + got_ref[...]
    part_ref[...] = part
    both_ref[:rows, :] = part
    both_ref[rows:, :] = rider_ref[...]


def quad_kernel(mine_ref, a_ref, b_ref, c_ref, part_ref):
    rows = mine_ref.shape[0]
    part_ref[...] = (mine_ref[...] + a_ref[:rows, :]) + (b_ref[...] + c_ref[...])


def small_call(kernel, shapes, *args, name):
    vmem = pl.BlockSpec(memory_space=pltpu.VMEM)
    return pl.pallas_call(
        kernel,
        out_shape=tuple(jax.ShapeDtypeStruct(shape, dtype) for shape, dtype in shapes),
        in_specs=[vmem] * len(args),
        out_specs=(vmem,) * len(shapes),
        compiler_params=pltpu.CompilerParams(vmem_limit_bytes=SMALL_LIMIT),
        name=name,
    )(*args)


def score_kernel(
    cap, examples, groups, chunk,
    part_ref, other_ref, scale_ref, diag_ref, test_ref, basis_ref, recv_hbm,
    out_hbm, self_ref,
    recv_ref, dir_ref, acc_ref, out_ref, tile_ref, ids_ref, recv_sem, ids_sem, out_sems,
):
    peers, feats, out_rows, _ = out_ref.shape
    tests_here = LANES // groups
    half = part_ref.shape[0] - 8
    tests = 2 * half
    tiles = dir_ref.shape[0]
    starts = list(range(0, tiles, chunk))
    bulk = pltpu.make_async_copy(recv_hbm, recv_ref, recv_sem)
    bulk.start()
    first = device_place(tiles)[1] == 0
    low = jnp.where(first, part_ref[...], other_ref[...])
    high = jnp.where(first, other_ref[...], part_ref[...])
    projection = jnp.concatenate([low[:half], high[:half]], axis=0)
    scaled = (scale_ref[...][None, :] * projection).astype(jnp.bfloat16)
    low_rank = jnp.sum(projection * scaled.astype(jnp.float32), axis=1, keepdims=True)
    eye = lax.broadcasted_iota(jnp.int32, (half, half), 0) == lax.broadcasted_iota(
        jnp.int32, (half, half), 1
    )
    diagonal = [
        jnp.sum(jnp.where(eye, piece[half : half + 1, :half], 0.0), axis=1, keepdims=True)
        for piece in (low, high)
    ]
    self_ref[...] = jnp.broadcast_to(
        low_rank + jnp.concatenate(diagonal, axis=0), (tests, LANES)
    )
    weights = scaled.T
    diag = diag_ref[...].T

    def directions(i):
        begin = starts[i]
        got = jnp.dot(
            basis_ref[begin * LANES : (begin + chunk) * LANES, :],
            weights,
            preferred_element_type=jnp.float32,
        )
        for tile in range(begin, begin + chunk):
            wide = test_ref[tile].astype(jnp.float32).T
            low_part = got[(tile - begin) * LANES : (tile - begin + 1) * LANES, :]
            dir_ref[tile] = (diag[:, tile : tile + 1] * wide + low_part).astype(jnp.bfloat16)

    early = len(starts) * 5 // 8
    for i in range(early):
        directions(i)
    bulk.wait()
    for peer in range(peers):
        row = recv_ref[peer, cap * examples :, :].astype(jnp.float32)
        tile_ref[peer : peer + 1, :] = row[:1, :].astype(jnp.int32)
    fetch = pltpu.make_async_copy(tile_ref, ids_ref, ids_sem)
    fetch.start()
    for i in range(early, len(starts)):
        directions(i)
    fetch.wait()

    waves, unroll = out_sems.shape[0], acc_ref.shape[0]

    def some_peers(step, carry):
        for i in range(unroll):
            peer = step * unroll + i
            for place in range(cap):
                acc_ref[i, place * examples : (place + 1) * examples, :] = jnp.dot(
                    recv_ref[peer, place * examples : (place + 1) * examples, :],
                    dir_ref[ids_ref[peer, place]],
                    preferred_element_type=jnp.float32,
                )
        for i in range(unroll):
            peer = step * unroll + i
            parts = [acc_ref[i, pl.ds(k, out_rows, stride=groups), :] for k in range(groups)]
            for feat in range(feats):
                lanes = slice(feat * tests_here, (feat + 1) * tests_here)
                out_ref[peer, feat] = jnp.concatenate(
                    [part[:, lanes] for part in parts], axis=1
                ).astype(jnp.bfloat16)
        return carry

    per_wave = peers // waves
    out_copies = []
    for i in range(waves):
        lax.fori_loop(i * per_wave // unroll, (i + 1) * per_wave // unroll, some_peers, 0)
        window = pl.ds(i * per_wave, per_wave)
        copy = pltpu.make_async_copy(out_ref.at[window], out_hbm.at[window], out_sems.at[i])
        copy.start()
        out_copies.append(copy)
    for copy in out_copies:
        copy.wait()


def xor_permute(value, axes, size, offset):
    return lax.ppermute(value, axes, [(i, i ^ offset) for i in range(size)])


def all_sum(mine, other, total, core_bit, rider):
    wide = jnp.float32
    got = xor_permute(other, BOTH, total, core_bit)
    shape = mine.shape
    (mine,) = small_call(hold_kernel, [(shape, wide)], mine, name="hold")
    part, send = small_call(
        pair_kernel,
        [(shape, wide), ((shape[0] + rider.shape[0], shape[1]), wide)],
        mine,
        got,
        rider,
        name="pair",
    )
    bits = [1 << b for b in range(total.bit_length() - 1) if (1 << b) != core_bit]
    arrived = None
    stages = [(bits[0], bits[1])] + [(bit, 0) for bit in bits[2:]]
    for low, high in stages:
        a = xor_permute(send if arrived is None else part, BOTH, total, low)
        if arrived is None:
            arrived = a[shape[0] :]
        if high:
            b = xor_permute(part, BOTH, total, high)
            c = xor_permute(part, BOTH, total, low | high)
        else:
            (part,) = small_call(add_kernel, [(shape, wide)], part, a, name="add")
            continue
        (part,) = small_call(quad_kernel, [(shape, wide)], part, a, b, c, name="quad")
    return part, xor_permute(part, BOTH, total, core_bit), arrived


def body(
    lanczos_basis,
    diagonal,
    lanczos_scale,
    test_tiles,
    test_values,
    train_tiles,
    train_count,
    train_values,
    resid_weight,
):
    ex_devices = lax.axis_size("ex")
    feat_devices = lax.axis_size("feat")
    total = ex_devices * feat_devices
    rank = lanczos_basis.shape[1]
    tiles_here = lanczos_basis.shape[0] // LANES
    test_count, test_slots = test_tiles.shape
    tests_here = test_count // feat_devices
    blocks_here, slots_here, examples, _ = train_values.shape
    slot_total = blocks_here * slots_here
    cap = max(2, (3 * slot_total + 2 * ex_devices - 1) // (2 * ex_devices))
    groups = LANES // tests_here
    rows_slot = examples // groups
    vmem = pl.BlockSpec(memory_space=pltpu.VMEM)
    smem = pl.BlockSpec(memory_space=pltpu.SMEM)
    hbm = pl.BlockSpec(memory_space=pltpu.HBM)
    params = pltpu.CompilerParams(vmem_limit_bytes=VMEM_LIMIT)

    sizes = (tiles_here * feat_devices, tiles_here, cap, examples, rows_slot)
    send_shape = (ex_devices, cap * examples + 8, LANES)
    send, want = pl.pallas_call(
        functools.partial(pack_kernel, sizes),
        out_shape=(
            jax.ShapeDtypeStruct(send_shape, jnp.bfloat16),
            jax.ShapeDtypeStruct((ex_devices, rank), jnp.float32),
        ),
        in_specs=[smem, smem, vmem],
        out_specs=(vmem, vmem),
        scratch_shapes=[pltpu.SMEM((ex_devices,), jnp.int32)],
        name="pack",
    )(train_tiles.T, train_count.T, train_values.reshape(slot_total * examples, LANES))
    recv = lax.all_to_all(send, "ex", split_axis=0, concat_axis=0, tiled=True)

    half = test_count // 2
    diag_tiles = diagonal.reshape(tiles_here, LANES)
    part_shape = (half + 8, rank)
    local_shape = (tiles_here, test_count, LANES)
    mine, other, local_test = pl.pallas_call(
        functools.partial(project_kernel, min(8, tiles_here) * LANES),
        out_shape=(
            jax.ShapeDtypeStruct(part_shape, jnp.float32),
            jax.ShapeDtypeStruct(part_shape, jnp.float32),
            jax.ShapeDtypeStruct(local_shape, jnp.bfloat16),
        ),
        in_specs=[hbm] * 4,
        out_specs=(hbm,) * 3,
        scratch_shapes=[
            pltpu.VMEM((test_slots, test_count), jnp.int32),
            pltpu.VMEM((tiles_here, LANES), jnp.float32),
            pltpu.VMEM((test_count * test_slots, LANES), jnp.bfloat16),
            pltpu.VMEM(lanczos_basis.shape, jnp.bfloat16),
            pltpu.VMEM(part_shape, jnp.float32),
            pltpu.VMEM(part_shape, jnp.float32),
            pltpu.VMEM(local_shape, jnp.bfloat16),
            pltpu.VMEM((test_count, tiles_here * LANES), jnp.bfloat16),
            pltpu.SemaphoreType.DMA((6,)),
            pltpu.SemaphoreType.DMA((tiles_here // min(8, tiles_here),)),
        ],
        name="project",
    )(
        test_tiles.T,
        diag_tiles,
        test_values.reshape(test_count * test_slots, LANES),
        lanczos_basis,
    )
    part, other, arrived = all_sum(mine, other, total, feat_devices, want)

    local_test, recv = lax.optimization_barrier((local_test, recv))

    out_shape = (ex_devices, feat_devices, cap * rows_slot, LANES)
    waves = min(4, ex_devices)
    scores, self_wide = pl.pallas_call(
        functools.partial(score_kernel, cap, examples, groups, min(4, tiles_here)),
        out_shape=(
            jax.ShapeDtypeStruct(out_shape, jnp.bfloat16),
            jax.ShapeDtypeStruct((test_count, LANES), jnp.float32),
        ),
        in_specs=[vmem] * 6 + [hbm],
        out_specs=(hbm, vmem),
        scratch_shapes=[
            pltpu.VMEM(send_shape, jnp.bfloat16),
            pltpu.VMEM((tiles_here, LANES, test_count), jnp.bfloat16),
            pltpu.VMEM((ex_devices // waves, cap * examples, test_count), jnp.float32),
            pltpu.VMEM(out_shape, jnp.bfloat16),
            pltpu.VMEM((ex_devices, LANES), jnp.int32),
            pltpu.SMEM((ex_devices, LANES), jnp.int32),
            pltpu.SemaphoreType.DMA,
            pltpu.SemaphoreType.DMA,
            pltpu.SemaphoreType.DMA((waves,)),
        ],
        compiler_params=params,
        name="scores",
    )(part, other, lanczos_scale, diag_tiles, local_test, lanczos_basis, recv)
    self_inf = self_wide[:, 0]
    scores = scores.reshape(total, cap * rows_slot, LANES)
    back = lax.all_to_all(scores, BOTH, split_axis=0, concat_axis=0, tiled=True)

    feat_index = lax.axis_index("feat")
    out_rows = cap * rows_slot
    want = want[:, :out_rows]
    if feat_devices == 2:
        theirs = arrived[:, :out_rows]
        mine_first = feat_index == 0
        table = jnp.stack(
            [jnp.where(mine_first, want, theirs), jnp.where(mine_first, theirs, want)], axis=1
        )
    else:
        table = lax.all_gather(want, "feat", axis=1)
    table = table.reshape(total * out_rows)
    places = jnp.arange(blocks_here * rows_slot, dtype=jnp.float32)
    onehot = (places[:, None] == table[None, :]).astype(jnp.bfloat16)
    raw = jnp.dot(
        onehot, back.reshape(total * cap * rows_slot, LANES), preferred_element_type=jnp.float32
    )
    raw = raw.reshape(blocks_here * rows_slot, groups, tests_here).transpose(2, 0, 1)
    raw = raw.reshape(tests_here, blocks_here * examples)
    self_mine = lax.dynamic_slice_in_dim(self_inf, feat_index * tests_here, tests_here)
    return -resid_weight[None, :] * raw / jnp.sqrt(self_mine)[:, None]


def solution(mesh):
    return jax.shard_map(
        body,
        mesh=mesh,
        in_specs=(
            P(("ex", "feat"), None),
            P(("ex", "feat")),
            P(),
            P(),
            P(),
            P("ex", "feat"),
            P("ex", "feat"),
            P("ex", "feat", None, None),
            P("ex"),
        ),
        out_specs=P("feat", "ex"),
        check_vma=False,
    )
```

```python
import functools

import jax
import jax.numpy as jnp
from jax import lax
from jax.experimental import pallas as pl
from jax.experimental.pallas import tpu as pltpu
from jax.sharding import PartitionSpec as P


LANES = 128
BOTH = ("ex", "feat")
VMEM_LIMIT = 16 << 20
SMALL_LIMIT = 4 << 20


def divide(value, by):
    if by & (by - 1) == 0:
        return lax.shift_right_logical(value, by.bit_length() - 1)
    return lax.div(value, by)


def pack_kernel(
    sizes, tiles_ref, count_ref, values_ref, send_ref, want_ref, fill_ref
):
    tiles_per_owner, tiles_here, cap, examples, rows_slot = sizes
    slots_here, blocks_here = tiles_ref.shape
    owners = send_ref.shape[0]
    rank = want_ref.shape[1]
    send_ref[...] = jnp.zeros_like(send_ref)
    for owner in range(owners):
        fill_ref[owner] = 0
    rows = lax.broadcasted_iota(jnp.int32, (owners, LANES), 0) * LANES
    lanes = lax.broadcasted_iota(jnp.int32, (owners, LANES), 1)
    id_key = rows + lanes
    want_key = rows + divide(lanes, rows_slot)
    want_low = (lanes - divide(lanes, rows_slot) * rows_slot).astype(jnp.float32)

    def one_block(block, carry):
        ids, want = carry
        count = count_ref[0, block]
        for slot in range(slots_here):
            tile = tiles_ref[slot, block]
            owner = divide(tile, tiles_per_owner)
            live = slot < count
            place = fill_ref[owner]
            fill_ref[owner] = place + live.astype(jnp.int32)
            start = pl.multiple_of(place * examples, examples)
            source = pl.multiple_of((block * slots_here + slot) * examples, examples)
            send_ref[owner, pl.ds(start, examples), :] = values_ref[pl.ds(source, examples), :]
            key = owner * LANES + place
            local = tile - divide(tile, tiles_here) * tiles_here
            ids = jnp.where(id_key == key, local.astype(jnp.float32), ids)
            want = jnp.where((want_key == key) & live, (block * rows_slot).astype(jnp.float32), want)
        return ids, want

    blank = jnp.full((owners, LANES), -float(LANES * LANES), jnp.float32)
    ids, want = lax.fori_loop(
        0, blocks_here, one_block, (jnp.zeros((owners, LANES), jnp.float32), blank)
    )
    for owner in range(owners):
        send_ref[owner, cap * examples :, :] = jnp.broadcast_to(
            ids[owner : owner + 1, :], (8, LANES)
        ).astype(jnp.bfloat16)
    want = jnp.where(want_key - rows < cap, want + want_low, blank)
    want_ref[...] = jnp.concatenate([want] + [blank] * (rank // LANES - 1), axis=1)


def device_place(tiles_here):
    ex, feat, feats = lax.axis_index("ex"), lax.axis_index("feat"), lax.axis_size("feat")
    return (ex * feats + feat) * tiles_here, ex % 2


def project_kernel(
    chunk, tests_hbm, diag_hbm, test_hbm, basis_hbm, mine_hbm, other_hbm, local_hbm,
    tests_ref, diag_ref, test_ref, basis_ref, mine_ref, other_ref, local_ref, flat_ref, sems, chunk_sems,
):
    small_copies = [
        pltpu.make_async_copy(source, target, sems.at[i])
        for i, (source, target) in enumerate(
            ((tests_hbm, tests_ref), (test_hbm, test_ref), (diag_hbm, diag_ref))
        )
    ]
    for copy in small_copies:
        copy.start()
    basis_copies = []
    for i in range(chunk_sems.shape[0]):
        window = pl.ds(i * chunk, chunk)
        copy = pltpu.make_async_copy(basis_hbm.at[window], basis_ref.at[window], chunk_sems.at[i])
        copy.start()
        basis_copies.append(copy)
    tiles_here = local_ref.shape[0]
    test_slots, tests = tests_ref.shape
    rank = basis_ref.shape[1]
    half = tests // 2
    first_tile, core = device_place(tiles_here)
    small_copies[0].wait()
    offset = tests_ref[...] - first_tile
    offset = jnp.where((offset >= 0) & (offset < tiles_here), offset, -1)
    offset = offset.astype(jnp.float32).T.astype(jnp.bfloat16)
    width = tests * test_slots
    column = lax.broadcasted_iota(jnp.int32, (test_slots, width), 1)
    spread = column - divide(column, test_slots) * test_slots == lax.broadcasted_iota(
        jnp.int32, (test_slots, width), 0
    )
    named = jnp.dot(
        offset, spread.astype(jnp.float32).astype(jnp.bfloat16), preferred_element_type=jnp.float32
    )
    own = divide(lax.broadcasted_iota(jnp.int32, (tests, width), 1), test_slots) == (
        lax.broadcasted_iota(jnp.int32, (tests, width), 0)
    )
    named = jnp.where(own, named, -1.0)
    small_copies[1].wait()
    small_copies[2].wait()
    influence = jnp.zeros((tests, LANES), jnp.float32)
    group = min(8, tiles_here)
    for begin in range(0, tiles_here, group):
        pick = jnp.concatenate(
            [
                jnp.where(named == float(tile), 1.0, 0.0).astype(jnp.bfloat16)
                for tile in range(begin, begin + group)
            ],
            axis=0,
        )
        got = jnp.dot(pick, test_ref[...], preferred_element_type=jnp.float32)
        for tile in range(begin, begin + group):
            wide = got[(tile - begin) * tests : (tile - begin + 1) * tests, :]
            narrow = wide.astype(jnp.bfloat16)
            local_ref[tile] = narrow
            flat_ref[:, tile * LANES : (tile + 1) * LANES] = narrow
            influence = influence + diag_ref[tile : tile + 1, :] * wide * wide

    local_copy = pltpu.make_async_copy(local_ref, local_hbm, sems.at[3])
    local_copy.start()
    projection = jnp.zeros((tests, rank), jnp.float32)
    for i, copy in enumerate(basis_copies):
        begin = i * chunk
        copy.wait()
        projection = projection + jnp.dot(
            flat_ref[:, begin : begin + chunk],
            basis_ref[begin : begin + chunk, :],
            preferred_element_type=jnp.float32,
        )
    total = jnp.sum(influence, axis=1, keepdims=True)
    eye = lax.broadcasted_iota(jnp.int32, (half, LANES), 0) == lax.broadcasted_iota(
        jnp.int32, (half, LANES), 1
    )
    row = [
        jnp.sum(jnp.where(eye, total[i * half : (i + 1) * half], 0.0), axis=0, keepdims=True)
        for i in range(2)
    ]
    first = core == 0
    out_copies = [local_copy]
    for ref, out_hbm, a, b in ((other_ref, other_hbm, 1, 0), (mine_ref, mine_hbm, 0, 1)):
        ref[:half, :] = jnp.where(
            first, projection[a * half : (a + 1) * half], projection[b * half : (b + 1) * half]
        )
        ref[half:, :] = jnp.zeros((8, rank), jnp.float32)
        ref[half : half + 1, :LANES] = jnp.where(first, row[a], row[b])
        copy = pltpu.make_async_copy(ref, out_hbm, sems.at[4 + a])
        copy.start()
        out_copies.append(copy)
    for copy in out_copies:
        copy.wait()


def add_kernel(mine_ref, got_ref, part_ref):
    part_ref[...] = mine_ref[...] + got_ref[...]


def hold_kernel(in_ref, out_ref):
    out_ref[...] = in_ref[...]


def pair_kernel(mine_ref, got_ref, rider_ref, part_ref, both_ref):
    rows = mine_ref.shape[0]
    part = mine_ref[...] + got_ref[...]
    part_ref[...] = part
    both_ref[:rows, :] = part
    both_ref[rows:, :] = rider_ref[...]


def quad_kernel(mine_ref, a_ref, b_ref, c_ref, part_ref):
    rows = mine_ref.shape[0]
    part_ref[...] = (mine_ref[...] + a_ref[:rows, :]) + (b_ref[...] + c_ref[...])


def small_call(kernel, shapes, *args, name):
    vmem = pl.BlockSpec(memory_space=pltpu.VMEM)
    return pl.pallas_call(
        kernel,
        out_shape=tuple(jax.ShapeDtypeStruct(shape, dtype) for shape, dtype in shapes),
        in_specs=[vmem] * len(args),
        out_specs=(vmem,) * len(shapes),
        compiler_params=pltpu.CompilerParams(vmem_limit_bytes=SMALL_LIMIT),
        name=name,
    )(*args)


def score_kernel(
    cap, examples, groups, chunk,
    part_ref, other_ref, scale_ref, diag_ref, test_hbm, basis_ref, recv_hbm,
    out_hbm, self_ref,
    test_ref, recv_ref, dir_ref, acc_ref, out_ref, tile_ref, ids_ref, test_sem, recv_sem, ids_sem, out_sems,
):
    peers, feats, out_rows, _ = out_ref.shape
    tests_here = LANES // groups
    half = part_ref.shape[0] - 8
    tests = 2 * half
    tiles = dir_ref.shape[0]
    starts = list(range(0, tiles, chunk))
    test_copy = pltpu.make_async_copy(test_hbm, test_ref, test_sem)
    test_copy.start()
    bulk = pltpu.make_async_copy(recv_hbm, recv_ref, recv_sem)
    bulk.start()
    first = device_place(tiles)[1] == 0
    low = jnp.where(first, part_ref[...], other_ref[...])
    high = jnp.where(first, other_ref[...], part_ref[...])
    projection = jnp.concatenate([low[:half], high[:half]], axis=0)
    scaled = (scale_ref[...][None, :] * projection).astype(jnp.bfloat16)
    low_rank = jnp.sum(projection * scaled.astype(jnp.float32), axis=1, keepdims=True)
    eye = lax.broadcasted_iota(jnp.int32, (half, half), 0) == lax.broadcasted_iota(
        jnp.int32, (half, half), 1
    )
    diagonal = [
        jnp.sum(jnp.where(eye, piece[half : half + 1, :half], 0.0), axis=1, keepdims=True)
        for piece in (low, high)
    ]
    self_ref[...] = jnp.broadcast_to(
        low_rank + jnp.concatenate(diagonal, axis=0), (tests, LANES)
    )
    weights = scaled.T
    diag = diag_ref[...].T

    def directions(i):
        begin = starts[i]
        got = jnp.dot(
            basis_ref[begin * LANES : (begin + chunk) * LANES, :],
            weights,
            preferred_element_type=jnp.float32,
        )
        for tile in range(begin, begin + chunk):
            wide = test_ref[tile].astype(jnp.float32).T
            low_part = got[(tile - begin) * LANES : (tile - begin + 1) * LANES, :]
            dir_ref[tile] = (diag[:, tile : tile + 1] * wide + low_part).astype(jnp.bfloat16)

    test_copy.wait()
    early = len(starts) * 5 // 8
    for i in range(early):
        directions(i)
    bulk.wait()
    for peer in range(peers):
        row = recv_ref[peer, cap * examples :, :].astype(jnp.float32)
        tile_ref[peer : peer + 1, :] = row[:1, :].astype(jnp.int32)
    fetch = pltpu.make_async_copy(tile_ref, ids_ref, ids_sem)
    fetch.start()
    for i in range(early, len(starts)):
        directions(i)
    fetch.wait()

    waves, unroll = out_sems.shape[0], acc_ref.shape[0]

    def some_peers(step, carry):
        for i in range(unroll):
            peer = step * unroll + i
            for place in range(cap):
                acc_ref[i, place * examples : (place + 1) * examples, :] = jnp.dot(
                    recv_ref[peer, place * examples : (place + 1) * examples, :],
                    dir_ref[ids_ref[peer, place]],
                    preferred_element_type=jnp.float32,
                )
        for i in range(unroll):
            peer = step * unroll + i
            parts = [acc_ref[i, pl.ds(k, out_rows, stride=groups), :] for k in range(groups)]
            for feat in range(feats):
                lanes = slice(feat * tests_here, (feat + 1) * tests_here)
                out_ref[peer, feat] = jnp.concatenate(
                    [part[:, lanes] for part in parts], axis=1
                ).astype(jnp.bfloat16)
        return carry

    per_wave = peers // waves
    out_copies = []
    for i in range(waves):
        lax.fori_loop(i * per_wave // unroll, (i + 1) * per_wave // unroll, some_peers, 0)
        window = pl.ds(i * per_wave, per_wave)
        copy = pltpu.make_async_copy(out_ref.at[window], out_hbm.at[window], out_sems.at[i])
        copy.start()
        out_copies.append(copy)
    for copy in out_copies:
        copy.wait()


def xor_permute(value, axes, size, offset):
    return lax.ppermute(value, axes, [(i, i ^ offset) for i in range(size)])


def all_sum(mine, other, total, core_bit, rider):
    wide = jnp.float32
    got = xor_permute(other, BOTH, total, core_bit)
    shape = mine.shape
    (mine,) = small_call(hold_kernel, [(shape, wide)], mine, name="hold")
    part, send = small_call(
        pair_kernel,
        [(shape, wide), ((shape[0] + rider.shape[0], shape[1]), wide)],
        mine,
        got,
        rider,
        name="pair",
    )
    bits = [1 << b for b in range(total.bit_length() - 1) if (1 << b) != core_bit]
    arrived = None
    stages = [(bits[0], bits[1])] + [(bit, 0) for bit in bits[2:]]
    for low, high in stages:
        a = xor_permute(send if arrived is None else part, BOTH, total, low)
        if arrived is None:
            arrived = a[shape[0] :]
        if high:
            b = xor_permute(part, BOTH, total, high)
            c = xor_permute(part, BOTH, total, low | high)
        else:
            (part,) = small_call(add_kernel, [(shape, wide)], part, a, name="add")
            continue
        (part,) = small_call(quad_kernel, [(shape, wide)], part, a, b, c, name="quad")
    return part, xor_permute(part, BOTH, total, core_bit), arrived


def body(
    lanczos_basis,
    diagonal,
    lanczos_scale,
    test_tiles,
    test_values,
    train_tiles,
    train_count,
    train_values,
    resid_weight,
):
    ex_devices = lax.axis_size("ex")
    feat_devices = lax.axis_size("feat")
    total = ex_devices * feat_devices
    rank = lanczos_basis.shape[1]
    tiles_here = lanczos_basis.shape[0] // LANES
    test_count, test_slots = test_tiles.shape
    tests_here = test_count // feat_devices
    blocks_here, slots_here, examples, _ = train_values.shape
    slot_total = blocks_here * slots_here
    cap = max(2, (3 * slot_total + 2 * ex_devices - 1) // (2 * ex_devices))
    groups = LANES // tests_here
    rows_slot = examples // groups
    vmem = pl.BlockSpec(memory_space=pltpu.VMEM)
    smem = pl.BlockSpec(memory_space=pltpu.SMEM)
    hbm = pl.BlockSpec(memory_space=pltpu.HBM)
    params = pltpu.CompilerParams(vmem_limit_bytes=VMEM_LIMIT)

    sizes = (tiles_here * feat_devices, tiles_here, cap, examples, rows_slot)
    send_shape = (ex_devices, cap * examples + 8, LANES)
    send, want = pl.pallas_call(
        functools.partial(pack_kernel, sizes),
        out_shape=(
            jax.ShapeDtypeStruct(send_shape, jnp.bfloat16),
            jax.ShapeDtypeStruct((ex_devices, rank), jnp.float32),
        ),
        in_specs=[smem, smem, vmem],
        out_specs=(vmem, vmem),
        scratch_shapes=[pltpu.SMEM((ex_devices,), jnp.int32)],
        name="pack",
    )(train_tiles.T, train_count.T, train_values.reshape(slot_total * examples, LANES))
    recv = lax.all_to_all(send, "ex", split_axis=0, concat_axis=0, tiled=True)

    half = test_count // 2
    diag_tiles = diagonal.reshape(tiles_here, LANES)
    part_shape = (half + 8, rank)
    local_shape = (tiles_here, test_count, LANES)
    mine, other, local_test = pl.pallas_call(
        functools.partial(project_kernel, min(16, tiles_here) * LANES),
        out_shape=(
            jax.ShapeDtypeStruct(part_shape, jnp.float32),
            jax.ShapeDtypeStruct(part_shape, jnp.float32),
            jax.ShapeDtypeStruct(local_shape, jnp.bfloat16),
        ),
        in_specs=[hbm] * 4,
        out_specs=(hbm,) * 3,
        scratch_shapes=[
            pltpu.VMEM((test_slots, test_count), jnp.int32),
            pltpu.VMEM((tiles_here, LANES), jnp.float32),
            pltpu.VMEM((test_count * test_slots, LANES), jnp.bfloat16),
            pltpu.VMEM(lanczos_basis.shape, jnp.bfloat16),
            pltpu.VMEM(part_shape, jnp.float32),
            pltpu.VMEM(part_shape, jnp.float32),
            pltpu.VMEM(local_shape, jnp.bfloat16),
            pltpu.VMEM((test_count, tiles_here * LANES), jnp.bfloat16),
            pltpu.SemaphoreType.DMA((6,)),
            pltpu.SemaphoreType.DMA((tiles_here // min(16, tiles_here),)),
        ],
        name="project",
    )(
        test_tiles.T,
        diag_tiles,
        test_values.reshape(test_count * test_slots, LANES),
        lanczos_basis,
    )
    part, other, arrived = all_sum(mine, other, total, feat_devices, want)

    local_test = pltpu.with_memory_space_constraint(local_test, pltpu.HBM)

    out_shape = (ex_devices, feat_devices, cap * rows_slot, LANES)
    waves = min(4, ex_devices)
    scores, self_wide = pl.pallas_call(
        functools.partial(score_kernel, cap, examples, groups, min(4, tiles_here)),
        out_shape=(
            jax.ShapeDtypeStruct(out_shape, jnp.bfloat16),
            jax.ShapeDtypeStruct((test_count, LANES), jnp.float32),
        ),
        in_specs=[vmem] * 4 + [hbm, vmem, hbm],
        out_specs=(hbm, vmem),
        scratch_shapes=[
            pltpu.VMEM(local_shape, jnp.bfloat16),
            pltpu.VMEM(send_shape, jnp.bfloat16),
            pltpu.VMEM((tiles_here, LANES, test_count), jnp.bfloat16),
            pltpu.VMEM((ex_devices // waves, cap * examples, test_count), jnp.float32),
            pltpu.VMEM(out_shape, jnp.bfloat16),
            pltpu.VMEM((ex_devices, LANES), jnp.int32),
            pltpu.SMEM((ex_devices, LANES), jnp.int32),
            pltpu.SemaphoreType.DMA,
            pltpu.SemaphoreType.DMA,
            pltpu.SemaphoreType.DMA,
            pltpu.SemaphoreType.DMA((waves,)),
        ],
        compiler_params=params,
        name="scores",
    )(part, other, lanczos_scale, diag_tiles, local_test, lanczos_basis, recv)
    self_inf = self_wide[:, 0]
    scores = scores.reshape(total, cap * rows_slot, LANES)
    back = lax.all_to_all(scores, BOTH, split_axis=0, concat_axis=0, tiled=True)

    feat_index = lax.axis_index("feat")
    out_rows = cap * rows_slot
    want = want[:, :out_rows]
    if feat_devices == 2:
        theirs = arrived[:, :out_rows]
        mine_first = feat_index == 0
        table = jnp.stack(
            [jnp.where(mine_first, want, theirs), jnp.where(mine_first, theirs, want)], axis=1
        )
    else:
        table = lax.all_gather(want, "feat", axis=1)
    table = table.reshape(total * out_rows)
    places = jnp.arange(blocks_here * rows_slot, dtype=jnp.float32)
    onehot = (places[:, None] == table[None, :]).astype(jnp.bfloat16)
    raw = jnp.dot(
        onehot, back.reshape(total * cap * rows_slot, LANES), preferred_element_type=jnp.float32
    )
    raw = raw.reshape(blocks_here * rows_slot, groups, tests_here).transpose(2, 0, 1)
    raw = raw.reshape(tests_here, blocks_here * examples)
    self_mine = lax.dynamic_slice_in_dim(self_inf, feat_index * tests_here, tests_here)
    return -resid_weight[None, :] * raw / jnp.sqrt(self_mine)[:, None]


def solution(mesh):
    return jax.shard_map(
        body,
        mesh=mesh,
        in_specs=(
            P(("ex", "feat"), None),
            P(("ex", "feat")),
            P(),
            P(),
            P(),
            P("ex", "feat"),
            P("ex", "feat"),
            P("ex", "feat", None, None),
            P("ex"),
        ),
        out_specs=P("feat", "ex"),
        check_vma=False,
    )
```
